128 devices in a mesh: energy: 32 (over x, z, core), mom: 4 (over y).
Axes of the slice: x: 4, y: 4, z: 4, core: 2. Of those that a mesh axis runs over, the one named last changes fastest.
Arguments:
- inverse_blocks: bfloat16 [2, 64, 4, 2048, 256], P(None, 'energy', 'mom'), may hold values from -0.25 to 0.25
- coupling_blocks: bfloat16 [2, 4, 2048, 256], P(None, 'mom'), may hold values from -0.10595703 to 0.10595703
- shifts: int32 [4], replicated, may hold values from 0 to 1, as said below
- emission_weight: float32 [4, 4, 4], replicated, may hold values from 0.5 to 4
- absorption_weight: float32 [4, 4, 4], replicated, may hold values from 0.5 to 4
- deform_potential: float32 [2048], replicated, may hold values from 0.5 to 2
- range_rows: int32 [128], replicated, may hold values from 1 to 32, 2048 in all
Outputs:
- sigma: bfloat16 [2, 64, 4, 2048, 256], P(None, 'energy', 'mom')
- charge: float32 [128], P(('energy', 'mom'))
The draws below stay inside these ranges and needn't reach their ends.
Inputs may be any that keep to these rules, and one draw needn't show every extreme that they name: `shifts`: one mode's shift is exactly 1. `range_rows`: the counts add up to 2048; the largest is exactly 32.
All inputs are finite; a program needn't handle non-finite values.
Results may differ from the reference program's by a relative error of at most 0.015.
Values may be sent and summed in bfloat16 or wider, within the bound.
A program may use at most 192 MiB of HBM per device.

```python
import math
import jax
import jax.numpy as jnp
import numpy as np
from jax import lax

B = 256
NB = 8
P_SIZE = 4
E = 64
K = 4
ROWS = 2048
ROWMAX = 32
SMAX = 1
DEVICES = 128


def draw_shifts(key, part):
    values = jax.random.randint(key, (P_SIZE,), 0, SMAX + 1)
    chosen = jax.random.randint(jax.random.fold_in(key, 7), (), 0, P_SIZE)
    return jnp.where(jnp.arange(P_SIZE) == chosen, SMAX, values).astype(jnp.int32)


def shard_levels(own_key, shape, pieces, least, high):
    loudness = 1.0
    for dim, shards_of in pieces:
        heights = jax.random.uniform(jax.random.fold_in(jax.random.fold_in(own_key, 6), dim), (shards_of,), jnp.float32, least / len(pieces), high / len(pieces))
        loudness = loudness * jnp.repeat(jnp.exp(heights), shape[dim] // shards_of).reshape((-1,) + (1,) * (len(shape) - 1 - dim))
    return loudness


def length_profile(number_of, total, most, lean):
    loads = [(1 << 20) // math.isqrt(standing ** lean) + 1 for standing in range(2, number_of + 1)]
    rest, holding = total - most - (number_of - 1), [1] * (number_of - 1)
    while rest > 0:
        candidates = [i for i in range(number_of - 1) if holding[i] < most]
        mass, budget = sum([loads[i] for i in candidates]), rest
        for i in candidates:
            addition = min(most - holding[i], max(1, budget * loads[i] // mass), rest)
            holding[i] = holding[i] + addition
            rest = rest - addition
    return np.array([most] + holding)


def ragged_sizes(key, amount, total, bound, lean):
    if amount == 2:
        one = jax.random.randint(key, (), max(1, total - bound), min(bound, total - 1) + 1)
        return jnp.stack([one, total - one])
    sizes = jnp.asarray(length_profile(amount, total, bound, lean), jnp.int32)
    pairs = (amount - 1) // 2
    donor, taker = sizes[1:1 + 2 * pairs:2], sizes[2:2 + 2 * pairs:2]
    room = jnp.minimum(donor - 1, bound - taker)
    moved = jax.random.randint(jax.random.fold_in(key, 1), (pairs,), 0, 1 << 20) % (room + 1)
    sizes = sizes.at[1:1 + 2 * pairs:2].set(donor - moved).at[2:2 + 2 * pairs:2].set(taker + moved)
    return sizes[jax.random.permutation(jax.random.fold_in(key, 2), amount)]


def normal_values(own_key, extent, deviation, limit, pieces=(), kind=jnp.bfloat16):
    level = shard_levels(own_key, extent, pieces, -0.22, 0.18) if pieces else 1.0
    entries = jax.random.normal(own_key, extent, jnp.float32) * deviation * level
    return jnp.minimum(jnp.maximum(entries, -limit), limit).astype(kind)


def setup_inputs(seed: int = 0) -> dict:
    splits = jax.random.split(jax.random.key(seed), 8)
    inverse_blocks = normal_values(splits[0], (2, E, K, ROWS, B), (2 * B) ** -0.5, 0.25, ((1, 32), (2, 4)))
    coupling_blocks = normal_values(splits[1], (2, K, ROWS, B), (0.4 / (2 * B) ** 0.5), 0.10595703, ((1, 4),))
    shifts = draw_shifts(jax.random.fold_in(splits[7], 71), 0)
    emission_weight = jnp.clip(jnp.exp(jax.random.uniform(splits[3], (P_SIZE, K, K), jnp.float32, math.log(0.5), math.log(4.0))), 0.5, 4.0)
    absorption_weight = jnp.clip(jnp.exp(jax.random.uniform(splits[4], (P_SIZE, K, K), jnp.float32, math.log(0.5), math.log(4.0))), 0.5, 4.0)
    deform_potential = jnp.clip(jnp.exp(jax.random.uniform(splits[5], (ROWS,), jnp.float32, math.log(0.5), math.log(2.0))), 0.5, 2.0)
    range_rows = ragged_sizes(splits[6], DEVICES, ROWS, ROWMAX, 2).astype(jnp.int32)
    return {"inverse_blocks": inverse_blocks, "coupling_blocks": coupling_blocks, "shifts": shifts, "emission_weight": emission_weight, "absorption_weight": absorption_weight, "deform_potential": deform_potential, "range_rows": range_rows}


HIGH = lax.Precision.HIGHEST


def rounded(value):
    return lax.optimization_barrier(value.astype(jnp.bfloat16)).astype(jnp.float32)


def complex_einsum(spec, left_re, left_im, right_re, right_im):
    def product(first, second):
        return jnp.einsum(spec, first, second, precision=HIGH)
    return (product(left_re, right_re) - product(left_im, right_im),
            product(left_re, right_im) + product(left_im, right_re))


def reference(inverse_blocks, coupling_blocks, shifts, emission_weight, absorption_weight, deform_potential, range_rows):
    inverse = inverse_blocks.astype(jnp.float32).reshape(2, E, K, NB, B, B)
    coupled = coupling_blocks.astype(jnp.float32).reshape(2, K, NB, B, B)
    row_parts = []
    sigma_parts = []
    green_re = None
    green_im = None
    for block in range(NB):
        a_re = inverse[0, :, :, block]
        a_im = inverse[1, :, :, block]
        t_re = coupled[0, :, block]
        t_im = coupled[1, :, block]
        if block == 0:
            s_re, s_im = complex_einsum('kij,klj->kil', t_re, t_im, t_re, -t_im)
            s_re = jnp.broadcast_to(rounded(s_re)[None], (E, K, B, B))
            s_im = jnp.broadcast_to(rounded(s_im)[None], (E, K, B, B))
        else:
            p_re, p_im = complex_einsum('kij,ekjl->ekil', t_re, t_im, green_re, green_im)
            p_re, p_im = rounded(p_re), rounded(p_im)
            s_re, s_im = complex_einsum('ekij,klj->ekil', p_re, p_im, t_re, -t_im)
            s_re, s_im = rounded(s_re), rounded(s_im)
        q_re, q_im = complex_einsum('ekij,ekjl->ekil', a_re, a_im, s_re, s_im)
        q_re, q_im = rounded(q_re), rounded(q_im)
        h_re, h_im = complex_einsum('ekij,ekjl->ekil', q_re, q_im, a_re, a_im)
        green_re = rounded(a_re + h_re)
        green_im = rounded(a_im + h_im)
        row_parts.append(-jnp.sum(jnp.diagonal(green_im, axis1=2, axis2=3), axis=(0, 1)))
        stacked = jnp.stack([green_re, green_im])
        padded = jnp.pad(stacked, ((0, 0), (SMAX, SMAX), (0, 0), (0, 0), (0, 0)))
        total = jnp.zeros((2, E, K, B, B), jnp.float32)
        for mode in range(P_SIZE):
            lower = lax.dynamic_slice_in_dim(padded, (SMAX - shifts[mode]).astype(jnp.int32), E, 1)
            upper = lax.dynamic_slice_in_dim(padded, (SMAX + shifts[mode]).astype(jnp.int32), E, 1)
            total = total + jnp.einsum('kq,zeqij->zekij', emission_weight[mode], lower, precision=HIGH)
            total = total + jnp.einsum('kq,zeqij->zekij', absorption_weight[mode], upper, precision=HIGH)
        scale = deform_potential[block * B:(block + 1) * B]
        sigma_parts.append((total * scale[:, None] * scale[None, :]).astype(jnp.bfloat16))
    sigma = jnp.stack(sigma_parts, axis=3).reshape(2, E, K, ROWS, B)
    density = jnp.concatenate(row_parts)
    starts = jnp.cumsum(range_rows) - range_rows
    row_ids = jnp.arange(ROWS, dtype=jnp.int32)
    member = (row_ids[:, None] >= starts[None, :]) & (row_ids[:, None] < (starts + range_rows)[None, :])
    charge = jnp.dot(density, member.astype(jnp.float32), precision=HIGH)
    return sigma, charge
```

```python
import jax
import jax.numpy as jnp
from jax import lax
from jax.experimental import pallas as pl
from jax.experimental.pallas import tpu as pltpu
from jax.sharding import PartitionSpec as P

MESH = pl.DeviceIdType.MESH
F32 = jnp.float32
BF16 = jnp.bfloat16
B = 256
NB = 8
EL = 2
K = 4
Q = B // K
NE = 32
NT = (((1,), (1,)), ((), ()))


def mm(left, right):
    return jnp.dot(left, right, preferred_element_type=F32)


def mm_nt(left, right):
    return lax.dot_general(left, right, NT, preferred_element_type=F32)


def kernel(a_hbm, t_hbm, d_hbm, shifts, emission, absorption, range_rows, sigma, charge,
           av, tv, dv, gb, rb, hlo, hhi, sb, lmat, dens, dsum, dpart,
           a_sem, t_sem, d_sem, gs_sem, gr_sem, hs_sem, hr_sem, ss_sem, sr_sem, own_sem, ds_sem, dr_sem):
    E = lax.axis_index("energy")
    me = lax.axis_index("mom")
    x, rest = E // 8, lax.rem(E, 8)
    z, core = rest // 2, lax.rem(rest, 2)

    def mom_peer(d):
        return (E, lax.rem(me + d, K))

    def z_peer(d):
        return (x * 8 + lax.rem(z + d, 4) * 2 + core, me)

    def x_peer(d):
        return (lax.rem(E + 8 * d, NE), me)

    above, below = (lax.rem(E + 1, NE), me), (lax.rem(E + NE - 1, NE), me)
    twin = (x * 8 + z * 2 + 1 - core, me)
    greeted = [mom_peer(d) for d in (1, 2, 3)] + [above, below, twin]
    greeted += [z_peer(d) for d in (1, 2, 3)] + [x_peer(d) for d in (1, 2, 3)]

    barrier = pltpu.get_barrier_semaphore()
    for peer in greeted:
        pl.semaphore_signal(barrier, inc=1, device_id=peer, device_id_type=MESH)

    def t_copy(i):
        return pltpu.make_async_copy(t_hbm.at[:, 0, pl.ds(i * B, B), :], tv.at[i], t_sem.at[i])

    def a_copy(i):
        return pltpu.make_async_copy(a_hbm.at[:, :, 0, pl.ds(i * B, B), :], av.at[i], a_sem.at[i])

    def d_copy(i):
        return pltpu.make_async_copy(d_hbm.at[pl.ds(i * B, B)], dv.at[i], d_sem.at[i])

    for i in range(NB):
        t_copy(i).start()
        a_copy(i).start()
    for i in range(NB):
        d_copy(i).start()

    def gather(i, d):
        return pltpu.make_async_remote_copy(
            gb.at[i, lax.rem(me + d, K)], rb.at[i, :, me], gs_sem.at[i, d - 1], gr_sem.at[i, d - 1],
            device_id=mom_peer(d), device_id_type=MESH)

    def gathered(i, d):
        source = lax.rem(me + K - d, K)
        return pltpu.make_async_remote_copy(
            gb.at[i, source], rb.at[i, :, source], gs_sem.at[i, d - 1], gr_sem.at[i, d - 1],
            device_id=mom_peer(d), device_id_type=MESH)

    def halo_up(i):
        return pltpu.make_async_remote_copy(
            rb.at[i, 1], hlo.at[i], hs_sem.at[i, 0], hr_sem.at[i, 0], device_id=above, device_id_type=MESH)

    def halo_down(i):
        return pltpu.make_async_remote_copy(
            rb.at[i, 0], hhi.at[i], hs_sem.at[i, 1], hr_sem.at[i, 1], device_id=below, device_id_type=MESH)

    def scatter(i, d):
        return pltpu.make_async_remote_copy(
            sb.at[i, lax.rem(me + d, K)], sigma.at[:, :, 0, pl.ds(i * B + me * Q, Q), :],
            ss_sem.at[i, d - 1], sr_sem.at[i, d - 1], device_id=mom_peer(d), device_id_type=MESH)

    def scattered(i, d):
        source = lax.rem(me + K - d, K)
        return pltpu.make_async_remote_copy(
            sb.at[i, source], sigma.at[:, :, 0, pl.ds(i * B + source * Q, Q), :],
            ss_sem.at[i, d - 1], sr_sem.at[i, d - 1], device_id=mom_peer(d), device_id_type=MESH)

    def own_copy(i):
        return pltpu.make_async_copy(
            sb.at[i, me], sigma.at[:, :, 0, pl.ds(i * B + me * Q, Q), :], own_sem.at[i])

    picked = [(shifts[p] == 1).astype(F32) for p in range(4)]
    not_first = (E > 0).astype(F32)
    not_last = (E < NE - 1).astype(F32)
    weight = {}
    for k in range(K):
        for q in range(K):
            low, mid, high = 0.0, 0.0, 0.0
            for p in range(4):
                em, ab = emission[p, k, q], absorption[p, k, q]
                low = low + picked[p] * em
                high = high + picked[p] * ab
                mid = mid + (1.0 - picked[p]) * (em + ab)
            weight[k, q] = (low, mid, high)
    row = lax.broadcasted_iota(jnp.int32, (16, B), 0)
    col = lax.broadcasted_iota(jnp.int32, (16, B), 1)
    group, same = col // 16, lax.rem(col, 16) == row
    for e in range(EL):
        for k in range(K):
            tile = jnp.zeros((16, B), F32)
            for part in range(3):
                source = e + part
                for q in range(K):
                    value = weight[k, q][part]
                    if source == 0:
                        value = value * not_first
                    if source == 3:
                        value = value * not_last
                    tile = jnp.where(group == source * K + q, value, tile)
            tile = jnp.where(same, tile, 0.0)
            top = tile.astype(BF16)
            at = (e * K + k) * 16
            lmat[at:at + 16, :] = top
            lmat[128 + at:128 + at + 16, :] = (tile - top.astype(F32)).astype(BF16)

    eye = lax.broadcasted_iota(jnp.int32, (B, B), 0) == lax.broadcasted_iota(jnp.int32, (B, B), 1)

    def rows_of(i, e, c):
        return gb[i, :, e, c].reshape(B, B)

    def solve(i, first):
        t_copy(i).wait()
        t_re, t_im = tv[i, 0], tv[i, 1]
        t_cat = jnp.concatenate([t_re, t_im], axis=1)
        t_swap = jnp.concatenate([-t_im, t_re], axis=1)
        if first:
            left = t_cat
        else:
            parts = []
            for e in range(EL):
                g_re, g_im = rows_of(i - 1, e, 0), rows_of(i - 1, e, 1)
                p_re = mm(t_cat, jnp.concatenate([g_re, -g_im], axis=0)).astype(BF16)
                p_im = mm(t_cat, jnp.concatenate([g_im, g_re], axis=0)).astype(BF16)
                parts.append(jnp.concatenate([p_re, p_im], axis=1))
            left = jnp.concatenate(parts, axis=0)
        s_re = mm_nt(left, t_cat).astype(BF16)
        s_im = mm_nt(left, t_swap).astype(BF16)
        a_copy(i).wait()
        trace = None
        for e in range(EL):
            at = 0 if first else e * B
            a_re, a_im = av[i, 0, e], av[i, 1, e]
            c_re, c_im = s_re[at:at + B], s_im[at:at + B]
            a_cat = jnp.concatenate([a_re, a_im], axis=1)
            q_re = mm(a_cat, jnp.concatenate([c_re, -c_im], axis=0)).astype(BF16)
            q_im = mm(a_cat, jnp.concatenate([c_im, c_re], axis=0)).astype(BF16)
            q_cat = jnp.concatenate([q_re, q_im], axis=1)
            h_re = mm(q_cat, jnp.concatenate([a_re, -a_im], axis=0))
            h_im = mm(q_cat, jnp.concatenate([a_im, a_re], axis=0))
            g_re = (a_re.astype(F32) + h_re).astype(BF16)
            g_im = (a_im.astype(F32) + h_im).astype(BF16)
            gb[i, :, e, 0] = g_re.reshape(K, Q, B)
            gb[i, :, e, 1] = g_im.reshape(K, Q, B)
            wide = g_im.astype(F32)
            trace = wide if trace is None else trace + wide
        dens[pl.ds(i, 1), :] = -jnp.sum(jnp.where(eye, trace, 0.0), axis=0, keepdims=True)

    def ship(i):
        for d in (1, 3, 2):
            gather(i, d).start()
        rb[i, :, me] = gb[i, me]

    solve(0, True)
    pl.semaphore_wait(barrier, len(greeted))
    ship(0)

    def chain(i, carry):
        solve(i, False)
        ship(i)
        return carry

    lax.fori_loop(1, NB, chain, 0)

    stages = [[mom_peer(d) for d in (1, 2, 3)], [twin], [z_peer(d) for d in (1, 2, 3)], [x_peer(d) for d in (1, 2, 3)]]

    def density_copy(stage, n):
        source = dens if stage == 0 else dsum.at[stage - 1]
        return pltpu.make_async_remote_copy(
            source, dpart.at[stage, n], ds_sem.at[stage, n], dr_sem.at[stage, n],
            device_id=stages[stage][n], device_id_type=MESH)

    def density_send(stage):
        for n in range(len(stages[stage])):
            density_copy(stage, n).start()

    def density_add(stage):
        total = dens[...] if stage == 0 else dsum[stage - 1]
        for n in range(len(stages[stage])):
            density_copy(stage, n).wait_recv()
            total = total + dpart[stage, n]
        dsum[stage] = total

    density_send(0)
    for i in range(NB):
        d_copy(i).wait()

    def mix(i):
        d_row = dv[pl.ds(i, 1), :]
        hit = (lax.broadcasted_iota(jnp.int32, (Q, B), 1)
               == lax.broadcasted_iota(jnp.int32, (Q, B), 0) + me * Q)
        d_col = jnp.sum(jnp.where(hit, d_row, 0.0), axis=1, keepdims=True)
        scale = d_col * d_row
        for c in range(2):
            for r in range(0, Q, 16):
                parts = [hlo[i, q, c, r:r + 16] for q in range(K)]
                for e in range(EL):
                    parts += [rb[i, e, q, c, r:r + 16] for q in range(K)]
                parts += [hhi[i, q, c, r:r + 16] for q in range(K)]
                out = mm(lmat[...], jnp.concatenate(parts, axis=0))
                out = (out[:128] + out[128:]).reshape(EL, K, 16, B) * scale[r:r + 16][None, None]
                out = out.astype(BF16)
                for e in range(EL):
                    for k in range(K):
                        sb[i, k, c, e, r:r + 16] = out[e, k]

    def step(i, carry):
        @pl.when(i < NB)
        def _():
            for d in (1, 2, 3):
                gathered(i, d).wait_recv()
            halo_up(i).start()
            halo_down(i).start()

        for stage in range(4):
            @pl.when(i == 2 + stage)
            def _(stage=stage):
                density_add(stage)
                if stage < 3:
                    density_send(stage + 1)

        @pl.when(i > 0)
        def _():
            halo_up(i - 1).wait_recv()
            halo_down(i - 1).wait_recv()
            mix(i - 1)
            for d in (1, 3, 2):
                scatter(i - 1, d).start()
            own_copy(i - 1).start()
        return carry

    lax.fori_loop(0, NB + 1, step, 0)

    device = E * K + me
    start = 0
    for n in range(NE * K):
        start = start + jnp.where(n < device, range_rows[n], 0)
    stop = start + range_rows[device]
    row_id = lax.broadcasted_iota(jnp.int32, (NB, B), 0) * B + lax.broadcasted_iota(jnp.int32, (NB, B), 1)
    inside = (row_id >= start) & (row_id < stop)
    charge[0] = jnp.sum(jnp.where(inside, dsum[3], 0.0))

    def finish(i, carry):
        for d in (1, 2, 3):
            gather(i, d).wait_send()
            scatter(i, d).wait_send()
            scattered(i, d).wait_recv()
        halo_up(i).wait_send()
        halo_down(i).wait_send()
        own_copy(i).wait()
        return carry

    lax.fori_loop(0, NB, finish, 0)
    for stage in range(4):
        for n in range(len(stages[stage])):
            density_copy(stage, n).wait_send()


def body(inverse_blocks, coupling_blocks, shifts, emission_weight, absorption_weight, deform_potential, range_rows):
    smem = pl.BlockSpec(memory_space=pltpu.SMEM)
    hbm = pl.BlockSpec(memory_space=pl.ANY)
    dma = pltpu.SemaphoreType.DMA
    return pl.pallas_call(
        kernel,
        out_shape=(
            jax.ShapeDtypeStruct(inverse_blocks.shape, BF16),
            jax.ShapeDtypeStruct((1,), F32),
        ),
        in_specs=[hbm, hbm, hbm, smem, smem, smem, smem],
        out_specs=(hbm, smem),
        scratch_shapes=[
            pltpu.VMEM((NB, 2, EL, B, B), BF16),
            pltpu.VMEM((NB, 2, B, B), BF16),
            pltpu.VMEM((NB, B), F32),
            pltpu.VMEM((NB, K, EL, 2, Q, B), BF16),
            pltpu.VMEM((NB, EL, K, 2, Q, B), BF16),
            pltpu.VMEM((NB, K, 2, Q, B), BF16),
            pltpu.VMEM((NB, K, 2, Q, B), BF16),
            pltpu.VMEM((NB, K, 2, EL, Q, B), BF16),
            pltpu.VMEM((B, B), BF16),
            pltpu.VMEM((NB, B), F32),
            pltpu.VMEM((4, NB, B), F32),
            pltpu.VMEM((4, 3, NB, B), F32),
            dma((NB,)), dma((NB,)), dma((NB,)),
            dma((NB, 3)), dma((NB, 3)),
            dma((NB, 2)), dma((NB, 2)),
            dma((NB, 3)), dma((NB, 3)),
            dma((NB,)),
            dma((4, 3)), dma((4, 3)),
        ],
        compiler_params=pltpu.CompilerParams(
            collective_id=0, has_side_effects=True, vmem_limit_bytes=48 << 20),
    )(inverse_blocks, coupling_blocks, deform_potential, shifts, emission_weight, absorption_weight, range_rows)


def solution(mesh):
    in_specs = (
        P(None, "energy", "mom", None, None),
        P(None, "mom", None, None),
        P(),
        P(),
        P(),
        P(),
        P(),
    )
    out_specs = (P(None, "energy", "mom", None, None), P(("energy", "mom")))
    return jax.shard_map(body, mesh=mesh, in_specs=in_specs, out_specs=out_specs, check_vma=False)
```

```python
import jax
import jax.numpy as jnp
from jax import lax
from jax.experimental import pallas as pl
from jax.experimental.pallas import tpu as pltpu
from jax.sharding import PartitionSpec as P

MESH = pl.DeviceIdType.MESH
F32 = jnp.float32
BF16 = jnp.bfloat16
B = 256
NB = 8
EL = 2
K = 4
Q = B // K
NE = 32
NT = (((1,), (1,)), ((), ()))


def mm(left, right):
    return jnp.dot(left, right, preferred_element_type=F32)


def mm_nt(left, right):
    return lax.dot_general(left, right, NT, preferred_element_type=F32)


def kernel(a_hbm, t_hbm, d_hbm, shifts_hbm, emission_hbm, absorption_hbm, range_hbm, sigma, charge,
           shifts, emission, absorption, range_rows, small_sem, av, tv, dv, gb, rb, hlo, hhi, sb, lmat, dens, dsum, dpart,
           a_sem, t_sem, d_sem, gs_sem, gr_sem, hs_sem, hr_sem, ss_sem, sr_sem, own_sem, ds_sem, dr_sem):
    E = lax.axis_index("energy")
    me = lax.axis_index("mom")
    x, rest = E // 8, lax.rem(E, 8)
    z, core = rest // 2, lax.rem(rest, 2)

    def mom_peer(d):
        return (E, lax.rem(me + d, K))

    def z_peer(d):
        return (x * 8 + lax.rem(z + d, 4) * 2 + core, me)

    def x_peer(d):
        return (lax.rem(E + 8 * d, NE), me)

    above, below = (lax.rem(E + 1, NE), me), (lax.rem(E + NE - 1, NE), me)
    twin = (x * 8 + z * 2 + 1 - core, me)
    greeted = [mom_peer(d) for d in (1, 2, 3)] + [above, below, twin]
    greeted += [z_peer(d) for d in (1, 2, 3)] + [x_peer(d) for d in (1, 2, 3)]

    barrier = pltpu.get_barrier_semaphore()
    for peer in greeted:
        pl.semaphore_signal(barrier, inc=1, device_id=peer, device_id_type=MESH)

    def t_copy(i):
        return pltpu.make_async_copy(t_hbm.at[:, 0, pl.ds(i * B, B), :], tv.at[i], t_sem.at[i])

    def a_copy(i):
        return pltpu.make_async_copy(a_hbm.at[:, :, 0, pl.ds(i * B, B), :], av.at[i], a_sem.at[i])

    def d_copy(i):
        return pltpu.make_async_copy(d_hbm.at[pl.ds(i * B, B)], dv.at[i], d_sem.at[i])

    small = ((shifts_hbm, shifts), (emission_hbm, emission), (absorption_hbm, absorption), (range_hbm, range_rows))
    for i in range(NB):
        t_copy(i).start()
        a_copy(i).start()
        if i == 0:
            for n, (source, target) in enumerate(small):
                pltpu.make_async_copy(source, target, small_sem.at[n]).start()
    for i in range(NB):
        d_copy(i).start()

    def gather(i, d):
        return pltpu.make_async_remote_copy(
            gb.at[i, lax.rem(me + d, K)], rb.at[i, :, me], gs_sem.at[i, d - 1], gr_sem.at[i, d - 1],
            device_id=mom_peer(d), device_id_type=MESH)

    def gathered(i, d):
        source = lax.rem(me + K - d, K)
        return pltpu.make_async_remote_copy(
            gb.at[i, source], rb.at[i, :, source], gs_sem.at[i, d - 1], gr_sem.at[i, d - 1],
            device_id=mom_peer(d), device_id_type=MESH)

    def halo_up(i):
        return pltpu.make_async_remote_copy(
            rb.at[i, 1], hlo.at[i], hs_sem.at[i, 0], hr_sem.at[i, 0], device_id=above, device_id_type=MESH)

    def halo_down(i):
        return pltpu.make_async_remote_copy(
            rb.at[i, 0], hhi.at[i], hs_sem.at[i, 1], hr_sem.at[i, 1], device_id=below, device_id_type=MESH)

    def scatter(i, d):
        return pltpu.make_async_remote_copy(
            sb.at[i, lax.rem(me + d, K)], sigma.at[:, :, 0, pl.ds(i * B + me * Q, Q), :],
            ss_sem.at[i, d - 1], sr_sem.at[i, d - 1], device_id=mom_peer(d), device_id_type=MESH)

    def scattered(i, d):
        source = lax.rem(me + K - d, K)
        return pltpu.make_async_remote_copy(
            sb.at[i, source], sigma.at[:, :, 0, pl.ds(i * B + source * Q, Q), :],
            ss_sem.at[i, d - 1], sr_sem.at[i, d - 1], device_id=mom_peer(d), device_id_type=MESH)

    def own_copy(i):
        return pltpu.make_async_copy(
            sb.at[i, me], sigma.at[:, :, 0, pl.ds(i * B + me * Q, Q), :], own_sem.at[i])

    eye = lax.broadcasted_iota(jnp.int32, (B, B), 0) == lax.broadcasted_iota(jnp.int32, (B, B), 1)

    def rows_of(i, e, c):
        return gb[i, :, e, c].reshape(B, B)

    def solve(i, first):
        t_copy(i).wait()
        t_re, t_im = tv[i, 0], tv[i, 1]
        t_cat = jnp.concatenate([t_re, t_im], axis=1)
        t_swap = jnp.concatenate([-t_im, t_re], axis=1)
        if first:
            left = t_cat
        else:
            parts = []
            for e in range(EL):
                g_re, g_im = rows_of(i - 1, e, 0), rows_of(i - 1, e, 1)
                p_re = mm(t_cat, jnp.concatenate([g_re, -g_im], axis=0)).astype(BF16)
                p_im = mm(t_cat, jnp.concatenate([g_im, g_re], axis=0)).astype(BF16)
                parts.append(jnp.concatenate([p_re, p_im], axis=1))
            left = jnp.concatenate(parts, axis=0)
        s_re = mm_nt(left, t_cat).astype(BF16)
        s_im = mm_nt(left, t_swap).astype(BF16)
        a_copy(i).wait()
        trace = None
        for e in range(EL):
            at = 0 if first else e * B
            a_re, a_im = av[i, 0, e], av[i, 1, e]
            c_re, c_im = s_re[at:at + B], s_im[at:at + B]
            a_cat = jnp.concatenate([a_re, a_im], axis=1)
            q_re = mm(a_cat, jnp.concatenate([c_re, -c_im], axis=0)).astype(BF16)
            q_im = mm(a_cat, jnp.concatenate([c_im, c_re], axis=0)).astype(BF16)
            q_cat = jnp.concatenate([q_re, q_im], axis=1)
            h_re = mm(q_cat, jnp.concatenate([a_re, -a_im], axis=0))
            h_im = mm(q_cat, jnp.concatenate([a_im, a_re], axis=0))
            g_re = (a_re.astype(F32) + h_re).astype(BF16)
            g_im = (a_im.astype(F32) + h_im).astype(BF16)
            gb[i, :, e, 0] = g_re.reshape(K, Q, B)
            gb[i, :, e, 1] = g_im.reshape(K, Q, B)
            wide = g_im.astype(F32)
            trace = wide if trace is None else trace + wide
        dens[pl.ds(i, 1), :] = -jnp.sum(jnp.where(eye, trace, 0.0), axis=0, keepdims=True)

    def ship(i):
        for d in (1, 3, 2):
            gather(i, d).start()
        rb[i, :, me] = gb[i, me]

    solve(0, True)
    pl.semaphore_wait(barrier, len(greeted))
    ship(0)

    for n, (source, target) in enumerate(small):
        pltpu.make_async_copy(source, target, small_sem.at[n]).wait()
    picked = [(shifts[p] == 1).astype(F32) for p in range(4)]
    not_first = (E > 0).astype(F32)
    not_last = (E < NE - 1).astype(F32)
    weight = {}
    for k in range(K):
        for q in range(K):
            low, mid, high = 0.0, 0.0, 0.0
            for p in range(4):
                em, ab = emission[p, k, q], absorption[p, k, q]
                low = low + picked[p] * em
                high = high + picked[p] * ab
                mid = mid + (1.0 - picked[p]) * (em + ab)
            weight[k, q] = (low, mid, high)
    row = lax.broadcasted_iota(jnp.int32, (16, B), 0)
    col = lax.broadcasted_iota(jnp.int32, (16, B), 1)
    group, same = col // 16, lax.rem(col, 16) == row
    for e in range(EL):
        for k in range(K):
            tile = jnp.zeros((16, B), F32)
            for part in range(3):
                source = e + part
                for q in range(K):
                    value = weight[k, q][part]
                    if source == 0:
                        value = value * not_first
                    if source == 3:
                        value = value * not_last
                    tile = jnp.where(group == source * K + q, value, tile)
            tile = jnp.where(same, tile, 0.0)
            top = tile.astype(BF16)
            at = (e * K + k) * 16
            lmat[at:at + 16, :] = top
            lmat[128 + at:128 + at + 16, :] = (tile - top.astype(F32)).astype(BF16)

    def chain(i, carry):
        solve(i, False)
        ship(i)
        return carry

    lax.fori_loop(1, NB, chain, 0)

    stages = [[mom_peer(d) for d in (1, 2, 3)], [twin], [z_peer(d) for d in (1, 2, 3)], [x_peer(d) for d in (1, 2, 3)]]

    def density_copy(stage, n):
        source = dens if stage == 0 else dsum.at[stage - 1]
        return pltpu.make_async_remote_copy(
            source, dpart.at[stage, n], ds_sem.at[stage, n], dr_sem.at[stage, n],
            device_id=stages[stage][n], device_id_type=MESH)

    def density_send(stage):
        for n in range(len(stages[stage])):
            density_copy(stage, n).start()

    def density_add(stage):
        total = dens[...] if stage == 0 else dsum[stage - 1]
        for n in range(len(stages[stage])):
            density_copy(stage, n).wait_recv()
            total = total + dpart[stage, n]
        dsum[stage] = total

    density_send(0)
    for i in range(NB):
        d_copy(i).wait()

    def mix(i):
        d_row = dv[pl.ds(i, 1), :]
        hit = (lax.broadcasted_iota(jnp.int32, (Q, B), 1)
               == lax.broadcasted_iota(jnp.int32, (Q, B), 0) + me * Q)
        d_col = jnp.sum(jnp.where(hit, d_row, 0.0), axis=1, keepdims=True)
        scale = d_col * d_row
        for c in range(2):
            for r in range(0, Q, 16):
                parts = [hlo[i, q, c, r:r + 16] for q in range(K)]
                for e in range(EL):
                    parts += [rb[i, e, q, c, r:r + 16] for q in range(K)]
                parts += [hhi[i, q, c, r:r + 16] for q in range(K)]
                out = mm(lmat[...], jnp.concatenate(parts, axis=0))
                out = (out[:128] + out[128:]).reshape(EL, K, 16, B) * scale[r:r + 16][None, None]
                out = out.astype(BF16)
                for e in range(EL):
                    for k in range(K):
                        sb[i, k, c, e, r:r + 16] = out[e, k]

    def step(i, carry):
        @pl.when(i < NB)
        def _():
            for d in (1, 2, 3):
                gathered(i, d).wait_recv()
            halo_up(i).start()
            halo_down(i).start()

        for stage in range(4):
            @pl.when(i == 2 + stage)
            def _(stage=stage):
                density_add(stage)
                if stage < 3:
                    density_send(stage + 1)

        @pl.when(i > 0)
        def _():
            halo_up(i - 1).wait_recv()
            halo_down(i - 1).wait_recv()
            mix(i - 1)
            for d in (1, 3, 2):
                scatter(i - 1, d).start()
            own_copy(i - 1).start()
        return carry

    lax.fori_loop(0, NB + 1, step, 0)

    device = E * K + me
    start = 0
    for n in range(NE * K):
        start = start + jnp.where(n < device, range_rows[n], 0)
    stop = start + range_rows[device]
    row_id = lax.broadcasted_iota(jnp.int32, (NB, B), 0) * B + lax.broadcasted_iota(jnp.int32, (NB, B), 1)
    inside = (row_id >= start) & (row_id < stop)
    charge[0] = jnp.sum(jnp.where(inside, dsum[3], 0.0))

    def finish(i, carry):
        for d in (1, 2, 3):
            gather(i, d).wait_send()
            scatter(i, d).wait_send()
            scattered(i, d).wait_recv()
        halo_up(i).wait_send()
        halo_down(i).wait_send()
        own_copy(i).wait()
        return carry

    lax.fori_loop(0, NB, finish, 0)
    for stage in range(4):
        for n in range(len(stages[stage])):
            density_copy(stage, n).wait_send()


def body(inverse_blocks, coupling_blocks, shifts, emission_weight, absorption_weight, deform_potential, range_rows):
    smem = pl.BlockSpec(memory_space=pltpu.SMEM)
    hbm = pl.BlockSpec(memory_space=pltpu.HBM)
    dma = pltpu.SemaphoreType.DMA
    return pl.pallas_call(
        kernel,
        out_shape=(
            jax.ShapeDtypeStruct(inverse_blocks.shape, BF16),
            jax.ShapeDtypeStruct((1,), F32),
        ),
        in_specs=[hbm] * 7,
        out_specs=(hbm, smem),
        scratch_shapes=[
            pltpu.SMEM((4,), jnp.int32),
            pltpu.SMEM((4, K, K), F32),
            pltpu.SMEM((4, K, K), F32),
            pltpu.SMEM((NE * K,), jnp.int32),
            dma((4,)),
            pltpu.VMEM((NB, 2, EL, B, B), BF16),
            pltpu.VMEM((NB, 2, B, B), BF16),
            pltpu.VMEM((NB, B), F32),
            pltpu.VMEM((NB, K, EL, 2, Q, B), BF16),
            pltpu.VMEM((NB, EL, K, 2, Q, B), BF16),
            pltpu.VMEM((NB, K, 2, Q, B), BF16),
            pltpu.VMEM((NB, K, 2, Q, B), BF16),
            pltpu.VMEM((NB, K, 2, EL, Q, B), BF16),
            pltpu.VMEM((B, B), BF16),
            pltpu.VMEM((NB, B), F32),
            pltpu.VMEM((4, NB, B), F32),
            pltpu.VMEM((4, 3, NB, B), F32),
            dma((NB,)), dma((NB,)), dma((NB,)),
            dma((NB, 3)), dma((NB, 3)),
            dma((NB, 2)), dma((NB, 2)),
            dma((NB, 3)), dma((NB, 3)),
            dma((NB,)),
            dma((4, 3)), dma((4, 3)),
        ],
        compiler_params=pltpu.CompilerParams(
            collective_id=0, has_side_effects=True, vmem_limit_bytes=48 << 20),
    )(*[pltpu.with_memory_space_constraint(v, pltpu.HBM) for v in (inverse_blocks, coupling_blocks, deform_potential, shifts, emission_weight, absorption_weight, range_rows)])


def solution(mesh):
    in_specs = (
        P(None, "energy", "mom", None, None),
        P(None, "mom", None, None),
        P(),
        P(),
        P(),
        P(),
        P(),
    )
    out_specs = (P(None, "energy", "mom", None, None), P(("energy", "mom")))
    return jax.shard_map(body, mesh=mesh, in_specs=in_specs, out_specs=out_specs, check_vma=False)
```

```python
import jax
import jax.numpy as jnp
from jax import lax
from jax.experimental import pallas as pl
from jax.experimental.pallas import tpu as pltpu
from jax.sharding import PartitionSpec as P

MESH = pl.DeviceIdType.MESH
F32 = jnp.float32
BF16 = jnp.bfloat16
B = 256
NB = 8
EL = 2
K = 4
Q = B // K
NE = 32
NT = (((1,), (1,)), ((), ()))


def mm(left, right):
    return jnp.dot(left, right, preferred_element_type=F32)


def mm_nt(left, right):
    return lax.dot_general(left, right, NT, preferred_element_type=F32)


def kernel(a_hbm, t_hbm, d_hbm, shifts_hbm, emission_hbm, absorption_hbm, range_hbm, sigma, charge,
           shifts, emission, absorption, range_rows, small_sem, av, tv, dv, gb, rb, hlo, hhi, sb, lmat, dens, dsum, dpart,
           a_sem, t_sem, d_sem, gs_sem, gr_sem, hs_sem, hr_sem, ss_sem, sr_sem, own_sem, ds_sem, dr_sem):
    E = lax.axis_index("energy")
    me = lax.axis_index("mom")
    x, rest = E // 8, lax.rem(E, 8)
    z, core = rest // 2, lax.rem(rest, 2)

    def mom_peer(d):
        return (E, lax.rem(me + d, K))

    def z_peer(d):
        return (x * 8 + lax.rem(z + d, 4) * 2 + core, me)

    def x_peer(d):
        return (lax.rem(E + 8 * d, NE), me)

    above, below = (lax.rem(E + 1, NE), me), (lax.rem(E + NE - 1, NE), me)
    twin = (x * 8 + z * 2 + 1 - core, me)
    greeted = [mom_peer(d) for d in (1, 2, 3)] + [above, below, twin]
    greeted += [z_peer(d) for d in (1, 2, 3)] + [x_peer(d) for d in (1, 2, 3)]

    barrier = pltpu.get_barrier_semaphore()
    for peer in greeted:
        pl.semaphore_signal(barrier, inc=1, device_id=peer, device_id_type=MESH)

    def t_copy(i):
        return pltpu.make_async_copy(t_hbm.at[:, 0, pl.ds(i * B, B), :], tv.at[i], t_sem.at[i])

    def a_copy(i):
        return pltpu.make_async_copy(a_hbm.at[:, :, 0, pl.ds(i * B, B), :], av.at[i], a_sem.at[i])

    def d_copy(i):
        return pltpu.make_async_copy(d_hbm.at[pl.ds(i * B, B)], dv.at[i], d_sem.at[i])

    small = ((shifts_hbm, shifts), (emission_hbm, emission), (absorption_hbm, absorption), (range_hbm, range_rows))
    for i in range(NB):
        t_copy(i).start()
        a_copy(i).start()
        if i == 0:
            for n, (source, target) in enumerate(small):
                pltpu.make_async_copy(source, target, small_sem.at[n]).start()
    for i in range(NB):
        d_copy(i).start()

    def gather(i, d):
        return pltpu.make_async_remote_copy(
            gb.at[i, lax.rem(me + d, K)], rb.at[i, :, me], gs_sem.at[i, d - 1], gr_sem.at[i, d - 1],
            device_id=mom_peer(d), device_id_type=MESH)

    def gathered(i, d):
        source = lax.rem(me + K - d, K)
        return pltpu.make_async_remote_copy(
            gb.at[i, source], rb.at[i, :, source], gs_sem.at[i, d - 1], gr_sem.at[i, d - 1],
            device_id=mom_peer(d), device_id_type=MESH)

    def halo_up(i):
        return pltpu.make_async_remote_copy(
            rb.at[i, 1], hlo.at[i], hs_sem.at[i, 0], hr_sem.at[i, 0], device_id=above, device_id_type=MESH)

    def halo_down(i):
        return pltpu.make_async_remote_copy(
            rb.at[i, 0], hhi.at[i], hs_sem.at[i, 1], hr_sem.at[i, 1], device_id=below, device_id_type=MESH)

    def scatter(i, d):
        return pltpu.make_async_remote_copy(
            sb.at[i, lax.rem(me + d, K)], sigma.at[:, :, 0, pl.ds(i * B + me * Q, Q), :],
            ss_sem.at[i, d - 1], sr_sem.at[i, d - 1], device_id=mom_peer(d), device_id_type=MESH)

    def scattered(i, d):
        source = lax.rem(me + K - d, K)
        return pltpu.make_async_remote_copy(
            sb.at[i, source], sigma.at[:, :, 0, pl.ds(i * B + source * Q, Q), :],
            ss_sem.at[i, d - 1], sr_sem.at[i, d - 1], device_id=mom_peer(d), device_id_type=MESH)

    def own_copy(i):
        return pltpu.make_async_copy(
            sb.at[i, me], sigma.at[:, :, 0, pl.ds(i * B + me * Q, Q), :], own_sem.at[i])

    eye = lax.broadcasted_iota(jnp.int32, (B, B), 0) == lax.broadcasted_iota(jnp.int32, (B, B), 1)

    def rows_of(i, e, c):
        return gb[i, :, e, c].reshape(B, B)

    def solve(i, first):
        t_copy(i).wait()
        t_re, t_im = tv[i, 0], tv[i, 1]
        t_cat = jnp.concatenate([t_re, t_im], axis=1)
        t_swap = jnp.concatenate([-t_im, t_re], axis=1)
        if first:
            left = t_cat
        else:
            parts = []
            for e in range(EL):
                g_re, g_im = rows_of(i - 1, e, 0), rows_of(i - 1, e, 1)
                p_re = mm(t_cat, jnp.concatenate([g_re, -g_im], axis=0)).astype(BF16)
                p_im = mm(t_cat, jnp.concatenate([g_im, g_re], axis=0)).astype(BF16)
                parts.append(jnp.concatenate([p_re, p_im], axis=1))
            left = jnp.concatenate(parts, axis=0)
        s_re = mm_nt(left, t_cat).astype(BF16)
        s_im = mm_nt(left, t_swap).astype(BF16)
        a_copy(i).wait()
        trace = None
        for e in range(EL):
            at = 0 if first else e * B
            a_re, a_im = av[i, 0, e], av[i, 1, e]
            c_re, c_im = s_re[at:at + B], s_im[at:at + B]
            a_cat = jnp.concatenate([a_re, a_im], axis=1)
            q_re = mm(a_cat, jnp.concatenate([c_re, -c_im], axis=0)).astype(BF16)
            q_im = mm(a_cat, jnp.concatenate([c_im, c_re], axis=0)).astype(BF16)
            q_cat = jnp.concatenate([q_re, q_im], axis=1)
            h_re = mm(q_cat, jnp.concatenate([a_re, -a_im], axis=0))
            h_im = mm(q_cat, jnp.concatenate([a_im, a_re], axis=0))
            g_re = (a_re.astype(F32) + h_re).astype(BF16)
            g_im = (a_im.astype(F32) + h_im).astype(BF16)
            gb[i, :, e, 0] = g_re.reshape(K, Q, B)
            gb[i, :, e, 1] = g_im.reshape(K, Q, B)
            wide = g_im.astype(F32)
            trace = wide if trace is None else trace + wide
        dens[pl.ds(i, 1), :] = -jnp.sum(jnp.where(eye, trace, 0.0), axis=0, keepdims=True)

    def ship(i):
        for d in (1, 3, 2):
            gather(i, d).start()
        rb[i, :, me] = gb[i, me]

    solve(0, True)
    pl.semaphore_wait(barrier, len(greeted))
    ship(0)

    for n, (source, target) in enumerate(small):
        pltpu.make_async_copy(source, target, small_sem.at[n]).wait()
    picked = [(shifts[p] == 1).astype(F32) for p in range(4)]
    not_first = (E > 0).astype(F32)
    not_last = (E < NE - 1).astype(F32)
    weight = {}
    for k in range(K):
        for q in range(K):
            low, mid, high = 0.0, 0.0, 0.0
            for p in range(4):
                em, ab = emission[p, k, q], absorption[p, k, q]
                low = low + picked[p] * em
                high = high + picked[p] * ab
                mid = mid + (1.0 - picked[p]) * (em + ab)
            weight[k, q] = (low, mid, high)
    row = lax.broadcasted_iota(jnp.int32, (16, B), 0)
    col = lax.broadcasted_iota(jnp.int32, (16, B), 1)
    group, same = col // 16, lax.rem(col, 16) == row
    for e in range(EL):
        for k in range(K):
            tile = jnp.zeros((16, B), F32)
            for part in range(3):
                source = e + part
                for q in range(K):
                    value = weight[k, q][part]
                    if source == 0:
                        value = value * not_first
                    if source == 3:
                        value = value * not_last
                    tile = jnp.where(group == source * K + q, value, tile)
            tile = jnp.where(same, tile, 0.0)
            top = tile.astype(BF16)
            at = (e * K + k) * 16
            lmat[at:at + 16, :] = top
            lmat[128 + at:128 + at + 16, :] = (tile - top.astype(F32)).astype(BF16)

    def chain(i, carry):
        solve(i, False)
        ship(i)
        return carry

    lax.fori_loop(1, NB, chain, 0)

    stages = [[mom_peer(d) for d in (1, 2, 3)], [twin], [z_peer(d) for d in (1, 2, 3)], [x_peer(d) for d in (1, 2, 3)]]

    def density_copy(stage, n):
        source = dens if stage == 0 else dsum.at[stage - 1]
        return pltpu.make_async_remote_copy(
            source, dpart.at[stage, n], ds_sem.at[stage, n], dr_sem.at[stage, n],
            device_id=stages[stage][n], device_id_type=MESH)

    def density_send(stage):
        for n in range(len(stages[stage])):
            density_copy(stage, n).start()

    def density_add(stage):
        total = dens[...] if stage == 0 else dsum[stage - 1]
        for n in range(len(stages[stage])):
            density_copy(stage, n).wait_recv()
            total = total + dpart[stage, n]
        dsum[stage] = total

    density_send(0)
    for i in range(NB):
        d_copy(i).wait()

    def mix(i):
        d_row = dv[pl.ds(i, 1), :]
        hit = (lax.broadcasted_iota(jnp.int32, (Q, B), 1)
               == lax.broadcasted_iota(jnp.int32, (Q, B), 0) + me * Q)
        d_col = jnp.sum(jnp.where(hit, d_row, 0.0), axis=1, keepdims=True)
        scale = d_col * d_row
        for c in range(2):
            for r in range(0, Q, 16):
                parts = [hlo[i, q, c, r:r + 16] for q in range(K)]
                for e in range(EL):
                    parts += [rb[i, e, q, c, r:r + 16] for q in range(K)]
                parts += [hhi[i, q, c, r:r + 16] for q in range(K)]
                out = mm(lmat[...], jnp.concatenate(parts, axis=0))
                out = (out[:128] + out[128:]).reshape(EL, K, 16, B) * scale[r:r + 16][None, None]
                out = out.astype(BF16)
                for e in range(EL):
                    for k in range(K):
                        sb[i, k, c, e, r:r + 16] = out[e, k]

    def step(i, carry):
        @pl.when(i < NB)
        def _():
            for d in (1, 2, 3):
                gathered(i, d).wait_recv()
            halo_up(i).start()
            halo_down(i).start()

        for stage in range(4):
            @pl.when(i == 2 + stage)
            def _(stage=stage):
                density_add(stage)
                if stage < 3:
                    density_send(stage + 1)

        @pl.when(i > 0)
        def _():
            halo_up(i - 1).wait_recv()
            halo_down(i - 1).wait_recv()
            mix(i - 1)
            for d in (1, 3, 2):
                scatter(i - 1, d).start()
            own_copy(i - 1).start()
        return carry

    lax.fori_loop(0, NB + 1, step, 0)

    device = E * K + me
    start = 0
    for n in range(NE * K):
        start = start + jnp.where(n < device, range_rows[n], 0)
    stop = start + range_rows[device]
    row_id = lax.broadcasted_iota(jnp.int32, (NB, B), 0) * B + lax.broadcasted_iota(jnp.int32, (NB, B), 1)
    inside = (row_id >= start) & (row_id < stop)
    charge[...] = jnp.full((1, 128), jnp.sum(jnp.where(inside, dsum[3], 0.0)), F32)

    def finish(i, carry):
        for d in (1, 2, 3):
            gather(i, d).wait_send()
            scatter(i, d).wait_send()
            scattered(i, d).wait_recv()
        halo_up(i).wait_send()
        halo_down(i).wait_send()
        own_copy(i).wait()
        return carry

    lax.fori_loop(0, NB, finish, 0)
    for stage in range(4):
        for n in range(len(stages[stage])):
            density_copy(stage, n).wait_send()


def place(landed, total, sigma, charge, sems):
    copies = [pltpu.make_async_copy(total, charge, sems.at[NB])]
    for i in range(4):
        copies.append(pltpu.make_async_copy(landed.at[i // 2, i % 2], sigma.at[i // 2, i % 2], sems.at[i]))
    for copy in copies:
        copy.start()
    for copy in copies:
        copy.wait()


def body(inverse_blocks, coupling_blocks, shifts, emission_weight, absorption_weight, deform_potential, range_rows):
    smem = pl.BlockSpec(memory_space=pltpu.SMEM)
    hbm = pl.BlockSpec(memory_space=pltpu.HBM)
    dma = pltpu.SemaphoreType.DMA
    landed, total = pl.pallas_call(
        kernel,
        out_shape=(
            jax.ShapeDtypeStruct(inverse_blocks.shape, BF16),
            jax.ShapeDtypeStruct((1, 128), F32),
        ),
        in_specs=[hbm] * 7,
        out_specs=(hbm, pl.BlockSpec(memory_space=pltpu.VMEM)),
        scratch_shapes=[
            pltpu.SMEM((4,), jnp.int32),
            pltpu.SMEM((4, K, K), F32),
            pltpu.SMEM((4, K, K), F32),
            pltpu.SMEM((NE * K,), jnp.int32),
            dma((4,)),
            pltpu.VMEM((NB, 2, EL, B, B), BF16),
            pltpu.VMEM((NB, 2, B, B), BF16),
            pltpu.VMEM((NB, B), F32),
            pltpu.VMEM((NB, K, EL, 2, Q, B), BF16),
            pltpu.VMEM((NB, EL, K, 2, Q, B), BF16),
            pltpu.VMEM((NB, K, 2, Q, B), BF16),
            pltpu.VMEM((NB, K, 2, Q, B), BF16),
            pltpu.VMEM((NB, K, 2, EL, Q, B), BF16),
            pltpu.VMEM((B, B), BF16),
            pltpu.VMEM((NB, B), F32),
            pltpu.VMEM((4, NB, B), F32),
            pltpu.VMEM((4, 3, NB, B), F32),
            dma((NB,)), dma((NB,)), dma((NB,)),
            dma((NB, 3)), dma((NB, 3)),
            dma((NB, 2)), dma((NB, 2)),
            dma((NB, 3)), dma((NB, 3)),
            dma((NB,)),
            dma((4, 3)), dma((4, 3)),
        ],
        compiler_params=pltpu.CompilerParams(
            collective_id=0, has_side_effects=True, vmem_limit_bytes=48 << 20),
    )(*[pltpu.with_memory_space_constraint(v, pltpu.HBM) for v in (inverse_blocks, coupling_blocks, deform_potential, shifts, emission_weight, absorption_weight, range_rows)])
    return pl.pallas_call(
        place,
        out_shape=(
            jax.ShapeDtypeStruct(landed.shape, BF16),
            jax.ShapeDtypeStruct((1,), F32),
        ),
        in_specs=[pl.BlockSpec(memory_space=pl.ANY)] * 2,
        out_specs=(hbm, hbm),
        scratch_shapes=[dma((NB + 1,))],
        compiler_params=pltpu.CompilerParams(vmem_limit_bytes=8 << 20),
    )(landed, total[0, :1])


def solution(mesh):
    in_specs = (
        P(None, "energy", "mom", None, None),
        P(None, "mom", None, None),
        P(),
        P(),
        P(),
        P(),
        P(),
    )
    out_specs = (P(None, "energy", "mom", None, None), P(("energy", "mom")))
    return jax.shard_map(body, mesh=mesh, in_specs=in_specs, out_specs=out_specs, check_vma=False)
```

```python
import jax
import jax.numpy as jnp
from jax import lax
from jax.experimental import pallas as pl
from jax.experimental.pallas import tpu as pltpu
from jax.sharding import PartitionSpec as P

MESH = pl.DeviceIdType.MESH
F32 = jnp.float32
BF16 = jnp.bfloat16
B = 256
NB = 8
EL = 2
K = 4
Q = B // K
NE = 32
NT = (((1,), (1,)), ((), ()))


def mm(left, right):
    return jnp.dot(left, right, preferred_element_type=F32)


def mm_nt(left, right):
    return lax.dot_general(left, right, NT, preferred_element_type=F32)


def kernel(a_hbm, t_hbm, d_hbm, shifts_hbm, emission_hbm, absorption_hbm, range_hbm, sigma, charge,
           shifts, emission, absorption, range_rows, small_sem, av, tv, dv, gb, rb, hlo, hhi, sb, lmat, dens, dsum, dpart,
           a_sem, t_sem, d_sem, gs_sem, gr_sem, hs_sem, hr_sem, ss_sem, sr_sem, own_sem, ds_sem, dr_sem, told):
    E = lax.axis_index("energy")
    me = lax.axis_index("mom")
    x, rest = E // 8, lax.rem(E, 8)
    z, core = rest // 2, lax.rem(rest, 2)

    def mom_peer(d):
        return (E, lax.rem(me + d, K))

    def z_peer(d):
        return (x * 8 + lax.rem(z + d, 4) * 2 + core, me)

    def x_peer(d):
        return (lax.rem(E + 8 * d, NE), me)

    above, below = (lax.rem(E + 1, NE), me), (lax.rem(E + NE - 1, NE), me)
    twin = (x * 8 + z * 2 + 1 - core, me)
    COUNTER, ENVOY = 1, 3
    is_counter, is_envoy = (me == COUNTER) & (core == 1), (me == ENVOY) & (core == 1)
    home = E - core
    rings = [(x * 8 + lax.rem(z + d, 4) * 2) for d in (1, 2, 3)] + [lax.rem(home + 8 * d, NE) for d in (1, 2, 3)]
    rings += [lax.rem(home + 2, NE), lax.rem(home + NE - 2, NE)]

    barrier = pltpu.get_barrier_semaphore()
    for d in (1, 2, 3):
        @pl.when((core == 0) | (lax.rem(me + d, K) != ENVOY))
        def _(d=d):
            pl.semaphore_signal(barrier, inc=1, device_id=mom_peer(d), device_id_type=MESH)

    @pl.when(core == 0)
    def _():
        pl.semaphore_signal(barrier, inc=1, device_id=(home + 1, COUNTER), device_id_type=MESH)

    def ring_ready():
        @pl.when(is_counter)
        def _():
            pl.semaphore_wait(barrier, 7)
            pl.semaphore_signal(told, inc=1, device_id=(E, ENVOY), device_id_type=MESH)

        @pl.when(is_envoy)
        def _():
            pl.semaphore_wait(told, 1)
            for ring in rings:
                pl.semaphore_signal(barrier, inc=1, device_id=(ring + 1, ENVOY), device_id_type=MESH)

        @pl.when(jnp.logical_not(is_counter | is_envoy))
        def _():
            pl.semaphore_wait(barrier, 3)

    def outside_ready():
        @pl.when(is_envoy)
        def _():
            pl.semaphore_wait(barrier, len(rings))
            for mom in range(K):
                pl.semaphore_signal(told, inc=1, device_id=(home, mom), device_id_type=MESH)
                if mom != ENVOY:
                    pl.semaphore_signal(told, inc=1, device_id=(home + 1, mom), device_id_type=MESH)

        @pl.when(jnp.logical_not(is_envoy))
        def _():
            pl.semaphore_wait(told, 1)

    def t_copy(i):
        return pltpu.make_async_copy(t_hbm.at[:, 0, pl.ds(i * B, B), :], tv.at[i], t_sem.at[i])

    def a_copy(i):
        return pltpu.make_async_copy(a_hbm.at[:, :, 0, pl.ds(i * B, B), :], av.at[i], a_sem.at[i])

    def d_copy(i):
        return pltpu.make_async_copy(d_hbm.at[pl.ds(i * B, B)], dv.at[i], d_sem.at[i])

    small = ((shifts_hbm, shifts), (emission_hbm, emission), (absorption_hbm, absorption), (range_hbm, range_rows))
    for i in range(NB):
        t_copy(i).start()
        a_copy(i).start()
        if i == 0:
            for n, (source, target) in enumerate(small):
                pltpu.make_async_copy(source, target, small_sem.at[n]).start()
    for i in range(NB):
        d_copy(i).start()

    def gather(i, d):
        return pltpu.make_async_remote_copy(
            gb.at[i, lax.rem(me + d, K)], rb.at[i, :, me], gs_sem.at[i, d - 1], gr_sem.at[i, d - 1],
            device_id=mom_peer(d), device_id_type=MESH)

    def gathered(i, d):
        source = lax.rem(me + K - d, K)
        return pltpu.make_async_remote_copy(
            gb.at[i, source], rb.at[i, :, source], gs_sem.at[i, d - 1], gr_sem.at[i, d - 1],
            device_id=mom_peer(d), device_id_type=MESH)

    def halo_up(i):
        return pltpu.make_async_remote_copy(
            rb.at[i, 1], hlo.at[i], hs_sem.at[i, 0], hr_sem.at[i, 0], device_id=above, device_id_type=MESH)

    def halo_down(i):
        return pltpu.make_async_remote_copy(
            rb.at[i, 0], hhi.at[i], hs_sem.at[i, 1], hr_sem.at[i, 1], device_id=below, device_id_type=MESH)

    def scatter(i, d):
        return pltpu.make_async_remote_copy(
            sb.at[i, lax.rem(me + d, K)], sigma.at[:, :, 0, pl.ds(i * B + me * Q, Q), :],
            ss_sem.at[i, d - 1], sr_sem.at[i, d - 1], device_id=mom_peer(d), device_id_type=MESH)

    def scattered(i, d):
        source = lax.rem(me + K - d, K)
        return pltpu.make_async_remote_copy(
            sb.at[i, source], sigma.at[:, :, 0, pl.ds(i * B + source * Q, Q), :],
            ss_sem.at[i, d - 1], sr_sem.at[i, d - 1], device_id=mom_peer(d), device_id_type=MESH)

    def own_copy(i):
        return pltpu.make_async_copy(
            sb.at[i, me], sigma.at[:, :, 0, pl.ds(i * B + me * Q, Q), :], own_sem.at[i])

    eye = lax.broadcasted_iota(jnp.int32, (B, B), 0) == lax.broadcasted_iota(jnp.int32, (B, B), 1)

    def rows_of(i, e, c):
        return gb[i, :, e, c].reshape(B, B)

    def note(i):
        wide = rows_of(i, 0, 1).astype(F32) + rows_of(i, 1, 1).astype(F32)
        dens[pl.ds(i, 1), :] = -jnp.sum(jnp.where(eye, wide, 0.0), axis=0, keepdims=True)

    def coupling(i):
        t_copy(i).wait()
        t_re, t_im = tv[i, 0], tv[i, 1]
        return jnp.concatenate([t_re, t_im], axis=1), jnp.concatenate([-t_im, t_re], axis=1)

    def first_block(c_re, c_im, quarters):
        def take(c, e):
            return jnp.concatenate([av[0, c, e, pl.ds(j * Q, Q)] for j in quarters], axis=0)

        height = len(quarters) * Q
        own = [(take(0, e), take(1, e)) for e in range(EL)]
        a_cat = jnp.concatenate([jnp.concatenate(pair, axis=1) for pair in own], axis=0)
        q_re = mm(a_cat, jnp.concatenate([c_re, -c_im], axis=0)).astype(BF16)
        q_im = mm(a_cat, jnp.concatenate([c_im, c_re], axis=0)).astype(BF16)
        for e in range(EL):
            at = e * height
            a_re, a_im = av[0, 0, e], av[0, 1, e]
            q_cat = jnp.concatenate([q_re[at:at + height], q_im[at:at + height]], axis=1)
            h_re = mm(q_cat, jnp.concatenate([a_re, -a_im], axis=0))
            h_im = mm(q_cat, jnp.concatenate([a_im, a_re], axis=0))
            for c, h in ((0, h_re), (1, h_im)):
                g = (own[e][c].astype(F32) + h).astype(BF16)
                for n, j in enumerate(quarters):
                    gb[0, j, e, c] = g[n * Q:(n + 1) * Q]

    def solve(i):
        t_cat, t_swap = coupling(i)
        parts = []
        for e in range(EL):
            g_re, g_im = rows_of(i - 1, e, 0), rows_of(i - 1, e, 1)
            p_re = mm(t_cat, jnp.concatenate([g_re, -g_im], axis=0)).astype(BF16)
            p_im = mm(t_cat, jnp.concatenate([g_im, g_re], axis=0)).astype(BF16)
            parts.append(jnp.concatenate([p_re, p_im], axis=1))
        left = jnp.concatenate(parts, axis=0)
        s_re = mm_nt(left, t_cat).astype(BF16)
        s_im = mm_nt(left, t_swap).astype(BF16)
        a_copy(i).wait()
        for e in range(EL):
            at = e * B
            a_re, a_im = av[i, 0, e], av[i, 1, e]
            c_re, c_im = s_re[at:at + B], s_im[at:at + B]
            a_cat = jnp.concatenate([a_re, a_im], axis=1)
            q_re = mm(a_cat, jnp.concatenate([c_re, -c_im], axis=0)).astype(BF16)
            q_im = mm(a_cat, jnp.concatenate([c_im, c_re], axis=0)).astype(BF16)
            q_cat = jnp.concatenate([q_re, q_im], axis=1)
            h_re = mm(q_cat, jnp.concatenate([a_re, -a_im], axis=0))
            h_im = mm(q_cat, jnp.concatenate([a_im, a_re], axis=0))
            gb[i, :, e, 0] = (a_re.astype(F32) + h_re).astype(BF16).reshape(K, Q, B)
            gb[i, :, e, 1] = (a_im.astype(F32) + h_im).astype(BF16).reshape(K, Q, B)
        note(i)

    def ship(i):
        for d in (1, 3, 2):
            gather(i, d).start()
        rb[i, :, me] = gb[i, me]

    t_cat, t_swap = coupling(0)
    c_re, c_im = mm_nt(t_cat, t_cat).astype(BF16), mm_nt(t_cat, t_swap).astype(BF16)
    a_copy(0).wait()
    near = 1 + 2 * lax.rem(me, 2)
    far = K - near
    first_block(c_re, c_im, [lax.rem(me + near, K)])
    ring_ready()
    gather(0, near).start()
    first_block(c_re, c_im, [lax.rem(me + far, K), lax.rem(me + 2, K), me])
    gather(0, far).start()
    gather(0, 2).start()
    rb[0, :, me] = gb[0, me]
    note(0)

    for n, (source, target) in enumerate(small):
        pltpu.make_async_copy(source, target, small_sem.at[n]).wait()
    picked = [(shifts[p] == 1).astype(F32) for p in range(4)]
    not_first = (E > 0).astype(F32)
    not_last = (E < NE - 1).astype(F32)
    weight = {}
    for k in range(K):
        for q in range(K):
            low, mid, high = 0.0, 0.0, 0.0
            for p in range(4):
                em, ab = emission[p, k, q], absorption[p, k, q]
                low = low + picked[p] * em
                high = high + picked[p] * ab
                mid = mid + (1.0 - picked[p]) * (em + ab)
            weight[k, q] = (low, mid, high)
    row = lax.broadcasted_iota(jnp.int32, (16, B), 0)
    col = lax.broadcasted_iota(jnp.int32, (16, B), 1)
    group, same = col // 16, lax.rem(col, 16) == row
    for e in range(EL):
        for k in range(K):
            tile = jnp.zeros((16, B), F32)
            for part in range(3):
                source = e + part
                for q in range(K):
                    value = weight[k, q][part]
                    if source == 0:
                        value = value * not_first
                    if source == 3:
                        value = value * not_last
                    tile = jnp.where(group == source * K + q, value, tile)
            tile = jnp.where(same, tile, 0.0)
            top = tile.astype(BF16)
            at = (e * K + k) * 16
            lmat[at:at + 16, :] = top
            lmat[128 + at:128 + at + 16, :] = (tile - top.astype(F32)).astype(BF16)

    def chain(i, carry):
        solve(i)
        ship(i)
        return carry

    lax.fori_loop(1, NB, chain, 0)
    outside_ready()

    stages = [[mom_peer(d) for d in (1, 2, 3)], [twin], [z_peer(d) for d in (1, 2, 3)], [x_peer(d) for d in (1, 2, 3)]]

    def density_copy(stage, n):
        source = dens if stage == 0 else dsum.at[stage - 1]
        return pltpu.make_async_remote_copy(
            source, dpart.at[stage, n], ds_sem.at[stage, n], dr_sem.at[stage, n],
            device_id=stages[stage][n], device_id_type=MESH)

    def density_send(stage):
        for n in range(len(stages[stage])):
            density_copy(stage, n).start()

    def density_add(stage):
        total = dens[...] if stage == 0 else dsum[stage - 1]
        for n in range(len(stages[stage])):
            density_copy(stage, n).wait_recv()
            total = total + dpart[stage, n]
        dsum[stage] = total

    density_send(0)
    for i in range(NB):
        d_copy(i).wait()

    def mix(i):
        d_row = dv[pl.ds(i, 1), :]
        hit = (lax.broadcasted_iota(jnp.int32, (Q, B), 1)
               == lax.broadcasted_iota(jnp.int32, (Q, B), 0) + me * Q)
        d_col = jnp.sum(jnp.where(hit, d_row, 0.0), axis=1, keepdims=True)
        scale = d_col * d_row
        for c in range(2):
            for r in range(0, Q, 16):
                parts = [hlo[i, q, c, r:r + 16] for q in range(K)]
                for e in range(EL):
                    parts += [rb[i, e, q, c, r:r + 16] for q in range(K)]
                parts += [hhi[i, q, c, r:r + 16] for q in range(K)]
                out = mm(lmat[...], jnp.concatenate(parts, axis=0))
                out = (out[:128] + out[128:]).reshape(EL, K, 16, B) * scale[r:r + 16][None, None]
                out = out.astype(BF16)
                for e in range(EL):
                    for k in range(K):
                        sb[i, k, c, e, r:r + 16] = out[e, k]

    def step(i, carry):
        @pl.when(i < NB)
        def _():
            for d in (1, 2, 3):
                gathered(i, d).wait_recv()
            halo_up(i).start()
            halo_down(i).start()

        for stage in range(4):
            @pl.when(i == 2 + stage)
            def _(stage=stage):
                density_add(stage)
                if stage < 3:
                    density_send(stage + 1)

        @pl.when(i > 0)
        def _():
            halo_up(i - 1).wait_recv()
            halo_down(i - 1).wait_recv()
            mix(i - 1)
            for d in (1, 3, 2):
                scatter(i - 1, d).start()
            own_copy(i - 1).start()
        return carry

    lax.fori_loop(0, NB + 1, step, 0)

    device = E * K + me
    start = 0
    for n in range(NE * K):
        start = start + jnp.where(n < device, range_rows[n], 0)
    stop = start + range_rows[device]
    row_id = lax.broadcasted_iota(jnp.int32, (NB, B), 0) * B + lax.broadcasted_iota(jnp.int32, (NB, B), 1)
    inside = (row_id >= start) & (row_id < stop)
    charge[...] = jnp.full((1, 128), jnp.sum(jnp.where(inside, dsum[3], 0.0)), F32)

    def finish(i, carry):
        for d in (1, 2, 3):
            gather(i, d).wait_send()
            scatter(i, d).wait_send()
            scattered(i, d).wait_recv()
        halo_up(i).wait_send()
        halo_down(i).wait_send()
        own_copy(i).wait()
        return carry

    lax.fori_loop(0, NB, finish, 0)
    for stage in range(4):
        for n in range(len(stages[stage])):
            density_copy(stage, n).wait_send()


def place(landed, total, sigma, charge, sems):
    copies = [pltpu.make_async_copy(total, charge, sems.at[NB])]
    for i in range(4):
        copies.append(pltpu.make_async_copy(landed.at[i // 2, i % 2], sigma.at[i // 2, i % 2], sems.at[i]))
    for copy in copies:
        copy.start()
    for copy in copies:
        copy.wait()


def body(inverse_blocks, coupling_blocks, shifts, emission_weight, absorption_weight, deform_potential, range_rows):
    smem = pl.BlockSpec(memory_space=pltpu.SMEM)
    hbm = pl.BlockSpec(memory_space=pltpu.HBM)
    dma = pltpu.SemaphoreType.DMA
    landed, total = pl.pallas_call(
        kernel,
        out_shape=(
            jax.ShapeDtypeStruct(inverse_blocks.shape, BF16),
            jax.ShapeDtypeStruct((1, 128), F32),
        ),
        in_specs=[hbm] * 7,
        out_specs=(hbm, pl.BlockSpec(memory_space=pltpu.VMEM)),
        scratch_shapes=[
            pltpu.SMEM((4,), jnp.int32),
            pltpu.SMEM((4, K, K), F32),
            pltpu.SMEM((4, K, K), F32),
            pltpu.SMEM((NE * K,), jnp.int32),
            dma((4,)),
            pltpu.VMEM((NB, 2, EL, B, B), BF16),
            pltpu.VMEM((NB, 2, B, B), BF16),
            pltpu.VMEM((NB, B), F32),
            pltpu.VMEM((NB, K, EL, 2, Q, B), BF16),
            pltpu.VMEM((NB, EL, K, 2, Q, B), BF16),
            pltpu.VMEM((NB, K, 2, Q, B), BF16),
            pltpu.VMEM((NB, K, 2, Q, B), BF16),
            pltpu.VMEM((NB, K, 2, EL, Q, B), BF16),
            pltpu.VMEM((B, B), BF16),
            pltpu.VMEM((NB, B), F32),
            pltpu.VMEM((4, NB, B), F32),
            pltpu.VMEM((4, 3, NB, B), F32),
            dma((NB,)), dma((NB,)), dma((NB,)),
            dma((NB, 3)), dma((NB, 3)),
            dma((NB, 2)), dma((NB, 2)),
            dma((NB, 3)), dma((NB, 3)),
            dma((NB,)),
            dma((4, 3)), dma((4, 3)),
            pltpu.SemaphoreType.REGULAR,
        ],
        compiler_params=pltpu.CompilerParams(
            collective_id=0, has_side_effects=True, vmem_limit_bytes=48 << 20),
    )(*[pltpu.with_memory_space_constraint(v, pltpu.HBM) for v in (inverse_blocks, coupling_blocks, deform_potential, shifts, emission_weight, absorption_weight, range_rows)])
    return pl.pallas_call(
        place,
        out_shape=(
            jax.ShapeDtypeStruct(landed.shape, BF16),
            jax.ShapeDtypeStruct((1,), F32),
        ),
        in_specs=[pl.BlockSpec(memory_space=pl.ANY)] * 2,
        out_specs=(hbm, hbm),
        scratch_shapes=[dma((NB + 1,))],
        compiler_params=pltpu.CompilerParams(vmem_limit_bytes=8 << 20),
    )(landed, total[0, :1])


def solution(mesh):
    in_specs = (
        P(None, "energy", "mom", None, None),
        P(None, "mom", None, None),
        P(),
        P(),
        P(),
        P(),
        P(),
    )
    out_specs = (P(None, "energy", "mom", None, None), P(("energy", "mom")))
    return jax.shard_map(body, mesh=mesh, in_specs=in_specs, out_specs=out_specs, check_vma=False)
```

```python
import jax
import jax.numpy as jnp
from jax import lax
from jax.experimental import pallas as pl
from jax.experimental.pallas import tpu as pltpu
from jax.sharding import PartitionSpec as P

MESH = pl.DeviceIdType.MESH
F32 = jnp.float32
BF16 = jnp.bfloat16
B = 256
NB = 8
EL = 2
K = 4
Q = B // K
NE = 32
NT = (((1,), (1,)), ((), ()))


def mm(left, right):
    return jnp.dot(left, right, preferred_element_type=F32)


def mm_nt(left, right):
    return lax.dot_general(left, right, NT, preferred_element_type=F32)


def kernel(a_hbm, t_hbm, d_hbm, shifts_hbm, emission_hbm, absorption_hbm, range_hbm, sigma, charge,
           shifts, emission, absorption, range_rows, small_sem, av, tv, dv, gb, rb, hlo, hhi, sb, lmat, dens, dsum, dpart,
           a_sem, t_sem, d_sem, gs_sem, gr_sem, hs_sem, hr_sem, ss_sem, sr_sem, own_sem, ds_sem, dr_sem, told):
    E = lax.axis_index("energy")
    me = lax.axis_index("mom")
    x, rest = E // 8, lax.rem(E, 8)
    z, core = rest // 2, lax.rem(rest, 2)

    def mom_peer(d):
        return (E, lax.rem(me + d, K))

    def z_peer(d):
        return (x * 8 + lax.rem(z + d, 4) * 2 + core, me)

    def x_peer(d):
        return (lax.rem(E + 8 * d, NE), me)

    above, below = (lax.rem(E + 1, NE), me), (lax.rem(E + NE - 1, NE), me)
    twin = (x * 8 + z * 2 + 1 - core, me)
    COUNTER, ENVOY = 0, 1
    is_counter, is_envoy = (me == COUNTER) & (core == 1), (me == ENVOY) & (core == 1)
    home = E - core
    rings = [(x * 8 + lax.rem(z + d, 4) * 2) for d in (1, 2, 3)] + [lax.rem(home + 8 * d, NE) for d in (1, 2, 3)]
    rings += [lax.rem(home + 2, NE), lax.rem(home + NE - 2, NE)]

    barrier = pltpu.get_barrier_semaphore()
    for d in (1, 2, 3):
        @pl.when((core == 0) | (lax.rem(me + d, K) != ENVOY))
        def _(d=d):
            pl.semaphore_signal(barrier, inc=1, device_id=mom_peer(d), device_id_type=MESH)

    @pl.when(core == 0)
    def _():
        pl.semaphore_signal(barrier, inc=1, device_id=(home + 1, COUNTER), device_id_type=MESH)

    def ring_ready():
        @pl.when(is_counter)
        def _():
            pl.semaphore_wait(barrier, 7)
            pl.semaphore_signal(told, inc=1, device_id=(E, ENVOY), device_id_type=MESH)

        @pl.when(is_envoy)
        def _():
            pl.semaphore_wait(told, 1)
            for ring in rings:
                pl.semaphore_signal(barrier, inc=1, device_id=(ring + 1, ENVOY), device_id_type=MESH)

        @pl.when(jnp.logical_not(is_counter | is_envoy))
        def _():
            pl.semaphore_wait(barrier, 3)

    def outside_ready():
        @pl.when(is_envoy)
        def _():
            pl.semaphore_wait(barrier, len(rings))
            for mom in range(K):
                pl.semaphore_signal(told, inc=1, device_id=(home, mom), device_id_type=MESH)
                if mom != ENVOY:
                    pl.semaphore_signal(told, inc=1, device_id=(home + 1, mom), device_id_type=MESH)

        @pl.when(jnp.logical_not(is_envoy))
        def _():
            pl.semaphore_wait(told, 1)

    def t_copy(i):
        return pltpu.make_async_copy(t_hbm.at[:, 0, pl.ds(i * B, B), :], tv.at[i], t_sem.at[i])

    def a_copy(i):
        return pltpu.make_async_copy(a_hbm.at[:, :, 0, pl.ds(i * B, B), :], av.at[i], a_sem.at[i])

    def d_copy(i):
        return pltpu.make_async_copy(d_hbm.at[pl.ds(i * B, B)], dv.at[i], d_sem.at[i])

    small = ((shifts_hbm, shifts), (emission_hbm, emission), (absorption_hbm, absorption), (range_hbm, range_rows))
    for i in range(NB):
        t_copy(i).start()
        a_copy(i).start()
        if i == 0:
            for n, (source, target) in enumerate(small):
                pltpu.make_async_copy(source, target, small_sem.at[n]).start()
    for i in range(NB):
        d_copy(i).start()

    def gather(i, d):
        return pltpu.make_async_remote_copy(
            gb.at[i, lax.rem(me + d, K)], rb.at[i, :, me], gs_sem.at[i, d - 1], gr_sem.at[i, d - 1],
            device_id=mom_peer(d), device_id_type=MESH)

    def gathered(i, d):
        source = lax.rem(me + K - d, K)
        return pltpu.make_async_remote_copy(
            gb.at[i, source], rb.at[i, :, source], gs_sem.at[i, d - 1], gr_sem.at[i, d - 1],
            device_id=mom_peer(d), device_id_type=MESH)

    def halo_up(i):
        return pltpu.make_async_remote_copy(
            rb.at[i, 1], hlo.at[i], hs_sem.at[i, 0], hr_sem.at[i, 0], device_id=above, device_id_type=MESH)

    def halo_down(i):
        return pltpu.make_async_remote_copy(
            rb.at[i, 0], hhi.at[i], hs_sem.at[i, 1], hr_sem.at[i, 1], device_id=below, device_id_type=MESH)

    def scatter(i, d):
        return pltpu.make_async_remote_copy(
            sb.at[i, lax.rem(me + d, K)], sigma.at[:, :, 0, pl.ds(i * B + me * Q, Q), :],
            ss_sem.at[i, d - 1], sr_sem.at[i, d - 1], device_id=mom_peer(d), device_id_type=MESH)

    def scattered(i, d):
        source = lax.rem(me + K - d, K)
        return pltpu.make_async_remote_copy(
            sb.at[i, source], sigma.at[:, :, 0, pl.ds(i * B + source * Q, Q), :],
            ss_sem.at[i, d - 1], sr_sem.at[i, d - 1], device_id=mom_peer(d), device_id_type=MESH)

    def own_copy(i):
        return pltpu.make_async_copy(
            sb.at[i, me], sigma.at[:, :, 0, pl.ds(i * B + me * Q, Q), :], own_sem.at[i])

    eye = lax.broadcasted_iota(jnp.int32, (B, B), 0) == lax.broadcasted_iota(jnp.int32, (B, B), 1)

    def rows_of(i, e, c):
        return gb[i, :, e, c].reshape(B, B)

    def note(i):
        wide = rows_of(i, 0, 1).astype(F32) + rows_of(i, 1, 1).astype(F32)
        dens[pl.ds(i, 1), :] = -jnp.sum(jnp.where(eye, wide, 0.0), axis=0, keepdims=True)

    def coupling(i):
        t_copy(i).wait()
        t_re, t_im = tv[i, 0], tv[i, 1]
        return jnp.concatenate([t_re, t_im], axis=1), jnp.concatenate([-t_im, t_re], axis=1)

    def first_block(c_re, c_im, quarters):
        def take(c, e):
            return jnp.concatenate([av[0, c, e, pl.ds(j * Q, Q)] for j in quarters], axis=0)

        height = len(quarters) * Q
        own = [(take(0, e), take(1, e)) for e in range(EL)]
        a_cat = jnp.concatenate([jnp.concatenate(pair, axis=1) for pair in own], axis=0)
        q_re = mm(a_cat, jnp.concatenate([c_re, -c_im], axis=0)).astype(BF16)
        q_im = mm(a_cat, jnp.concatenate([c_im, c_re], axis=0)).astype(BF16)
        for e in range(EL):
            at = e * height
            a_re, a_im = av[0, 0, e], av[0, 1, e]
            q_cat = jnp.concatenate([q_re[at:at + height], q_im[at:at + height]], axis=1)
            h_re = mm(q_cat, jnp.concatenate([a_re, -a_im], axis=0))
            h_im = mm(q_cat, jnp.concatenate([a_im, a_re], axis=0))
            for c, h in ((0, h_re), (1, h_im)):
                g = (own[e][c].astype(F32) + h).astype(BF16)
                for n, j in enumerate(quarters):
                    gb[0, j, e, c] = g[n * Q:(n + 1) * Q]

    def solve(i):
        t_cat, t_swap = coupling(i)
        parts = []
        for e in range(EL):
            g_re, g_im = rows_of(i - 1, e, 0), rows_of(i - 1, e, 1)
            p_re = mm(t_cat, jnp.concatenate([g_re, -g_im], axis=0)).astype(BF16)
            p_im = mm(t_cat, jnp.concatenate([g_im, g_re], axis=0)).astype(BF16)
            parts.append(jnp.concatenate([p_re, p_im], axis=1))
        left = jnp.concatenate(parts, axis=0)
        s_re = mm_nt(left, t_cat).astype(BF16)
        s_im = mm_nt(left, t_swap).astype(BF16)
        a_copy(i).wait()
        for e in range(EL):
            at = e * B
            a_re, a_im = av[i, 0, e], av[i, 1, e]
            c_re, c_im = s_re[at:at + B], s_im[at:at + B]
            a_cat = jnp.concatenate([a_re, a_im], axis=1)
            q_re = mm(a_cat, jnp.concatenate([c_re, -c_im], axis=0)).astype(BF16)
            q_im = mm(a_cat, jnp.concatenate([c_im, c_re], axis=0)).astype(BF16)
            q_cat = jnp.concatenate([q_re, q_im], axis=1)
            h_re = mm(q_cat, jnp.concatenate([a_re, -a_im], axis=0))
            h_im = mm(q_cat, jnp.concatenate([a_im, a_re], axis=0))
            gb[i, :, e, 0] = (a_re.astype(F32) + h_re).astype(BF16).reshape(K, Q, B)
            gb[i, :, e, 1] = (a_im.astype(F32) + h_im).astype(BF16).reshape(K, Q, B)
        note(i)

    def ship(i):
        for d in (1, 3, 2):
            gather(i, d).start()
        rb[i, :, me] = gb[i, me]

    t_cat, t_swap = coupling(0)
    c_re, c_im = mm_nt(t_cat, t_cat).astype(BF16), mm_nt(t_cat, t_swap).astype(BF16)
    a_copy(0).wait()
    near = 1 + 2 * lax.rem(me, 2)
    far = K - near
    first_block(c_re, c_im, [lax.rem(me + near, K)])
    ring_ready()
    gather(0, near).start()
    first_block(c_re, c_im, [lax.rem(me + far, K), lax.rem(me + 2, K), me])
    gather(0, far).start()
    gather(0, 2).start()
    rb[0, :, me] = gb[0, me]
    note(0)

    for n, (source, target) in enumerate(small):
        pltpu.make_async_copy(source, target, small_sem.at[n]).wait()
    picked = [(shifts[p] == 1).astype(F32) for p in range(4)]
    not_first = (E > 0).astype(F32)
    not_last = (E < NE - 1).astype(F32)
    weight = {}
    for k in range(K):
        for q in range(K):
            low, mid, high = 0.0, 0.0, 0.0
            for p in range(4):
                em, ab = emission[p, k, q], absorption[p, k, q]
                low = low + picked[p] * em
                high = high + picked[p] * ab
                mid = mid + (1.0 - picked[p]) * (em + ab)
            weight[k, q] = (low, mid, high)
    row = lax.broadcasted_iota(jnp.int32, (16, B), 0)
    col = lax.broadcasted_iota(jnp.int32, (16, B), 1)
    group, same = col // 16, lax.rem(col, 16) == row
    for e in range(EL):
        for k in range(K):
            tile = jnp.zeros((16, B), F32)
            for part in range(3):
                source = e + part
                for q in range(K):
                    value = weight[k, q][part]
                    if source == 0:
                        value = value * not_first
                    if source == 3:
                        value = value * not_last
                    tile = jnp.where(group == source * K + q, value, tile)
            tile = jnp.where(same, tile, 0.0)
            top = tile.astype(BF16)
            at = (e * K + k) * 16
            lmat[at:at + 16, :] = top
            lmat[128 + at:128 + at + 16, :] = (tile - top.astype(F32)).astype(BF16)

    def chain(i, carry):
        solve(i)
        ship(i)
        return carry

    lax.fori_loop(1, NB, chain, 0)
    outside_ready()

    stages = [[mom_peer(d) for d in (1, 2, 3)], [twin], [z_peer(d) for d in (1, 2, 3)], [x_peer(d) for d in (1, 2, 3)]]

    def density_copy(stage, n):
        source = dens if stage == 0 else dsum.at[stage - 1]
        return pltpu.make_async_remote_copy(
            source, dpart.at[stage, n], ds_sem.at[stage, n], dr_sem.at[stage, n],
            device_id=stages[stage][n], device_id_type=MESH)

    def density_send(stage):
        for n in range(len(stages[stage])):
            density_copy(stage, n).start()

    def density_add(stage):
        total = dens[...] if stage == 0 else dsum[stage - 1]
        for n in range(len(stages[stage])):
            density_copy(stage, n).wait_recv()
            total = total + dpart[stage, n]
        dsum[stage] = total

    density_send(0)
    for i in range(NB):
        d_copy(i).wait()

    def mix(i):
        d_row = dv[pl.ds(i, 1), :]
        hit = (lax.broadcasted_iota(jnp.int32, (Q, B), 1)
               == lax.broadcasted_iota(jnp.int32, (Q, B), 0) + me * Q)
        d_col = jnp.sum(jnp.where(hit, d_row, 0.0), axis=1, keepdims=True)
        scale = d_col * d_row
        for c in range(2):
            for r in range(0, Q, 16):
                parts = [hlo[i, q, c, r:r + 16] for q in range(K)]
                for e in range(EL):
                    parts += [rb[i, e, q, c, r:r + 16] for q in range(K)]
                parts += [hhi[i, q, c, r:r + 16] for q in range(K)]
                out = mm(lmat[...], jnp.concatenate(parts, axis=0))
                out = (out[:128] + out[128:]).reshape(EL, K, 16, B) * scale[r:r + 16][None, None]
                out = out.astype(BF16)
                for e in range(EL):
                    for k in range(K):
                        sb[i, k, c, e, r:r + 16] = out[e, k]

    def step(i, carry):
        @pl.when(i < NB)
        def _():
            for d in (1, 2, 3):
                gathered(i, d).wait_recv()
            halo_up(i).start()
            halo_down(i).start()

        for stage in range(4):
            @pl.when(i == 2 + stage)
            def _(stage=stage):
                density_add(stage)
                if stage < 3:
                    density_send(stage + 1)

        @pl.when(i > 0)
        def _():
            halo_up(i - 1).wait_recv()
            halo_down(i - 1).wait_recv()
            mix(i - 1)
            for d in (1, 3, 2):
                scatter(i - 1, d).start()
            own_copy(i - 1).start()
        return carry

    lax.fori_loop(0, NB + 1, step, 0)

    device = E * K + me
    start = 0
    for n in range(NE * K):
        start = start + jnp.where(n < device, range_rows[n], 0)
    stop = start + range_rows[device]
    row_id = lax.broadcasted_iota(jnp.int32, (NB, B), 0) * B + lax.broadcasted_iota(jnp.int32, (NB, B), 1)
    inside = (row_id >= start) & (row_id < stop)
    charge[...] = jnp.full((1, 128), jnp.sum(jnp.where(inside, dsum[3], 0.0)), F32)

    def finish(i, carry):
        for d in (1, 2, 3):
            gather(i, d).wait_send()
            scatter(i, d).wait_send()
            scattered(i, d).wait_recv()
        halo_up(i).wait_send()
        halo_down(i).wait_send()
        own_copy(i).wait()
        return carry

    lax.fori_loop(0, NB, finish, 0)
    for stage in range(4):
        for n in range(len(stages[stage])):
            density_copy(stage, n).wait_send()


def place(landed, total, sigma, charge, sems):
    copies = [pltpu.make_async_copy(total, charge, sems.at[NB])]
    for i in range(4):
        copies.append(pltpu.make_async_copy(landed.at[i // 2, i % 2], sigma.at[i // 2, i % 2], sems.at[i]))
    for copy in copies:
        copy.start()
    for copy in copies:
        copy.wait()


def body(inverse_blocks, coupling_blocks, shifts, emission_weight, absorption_weight, deform_potential, range_rows):
    smem = pl.BlockSpec(memory_space=pltpu.SMEM)
    hbm = pl.BlockSpec(memory_space=pltpu.HBM)
    dma = pltpu.SemaphoreType.DMA
    landed, total = pl.pallas_call(
        kernel,
        out_shape=(
            jax.ShapeDtypeStruct(inverse_blocks.shape, BF16),
            jax.ShapeDtypeStruct((1, 128), F32),
        ),
        in_specs=[hbm] * 7,
        out_specs=(hbm, pl.BlockSpec(memory_space=pltpu.VMEM)),
        scratch_shapes=[
            pltpu.SMEM((4,), jnp.int32),
            pltpu.SMEM((4, K, K), F32),
            pltpu.SMEM((4, K, K), F32),
            pltpu.SMEM((NE * K,), jnp.int32),
            dma((4,)),
            pltpu.VMEM((NB, 2, EL, B, B), BF16),
            pltpu.VMEM((NB, 2, B, B), BF16),
            pltpu.VMEM((NB, B), F32),
            pltpu.VMEM((NB, K, EL, 2, Q, B), BF16),
            pltpu.VMEM((NB, EL, K, 2, Q, B), BF16),
            pltpu.VMEM((NB, K, 2, Q, B), BF16),
            pltpu.VMEM((NB, K, 2, Q, B), BF16),
            pltpu.VMEM((NB, K, 2, EL, Q, B), BF16),
            pltpu.VMEM((B, B), BF16),
            pltpu.VMEM((NB, B), F32),
            pltpu.VMEM((4, NB, B), F32),
            pltpu.VMEM((4, 3, NB, B), F32),
            dma((NB,)), dma((NB,)), dma((NB,)),
            dma((NB, 3)), dma((NB, 3)),
            dma((NB, 2)), dma((NB, 2)),
            dma((NB, 3)), dma((NB, 3)),
            dma((NB,)),
            dma((4, 3)), dma((4, 3)),
            pltpu.SemaphoreType.REGULAR,
        ],
        compiler_params=pltpu.CompilerParams(
            collective_id=0, has_side_effects=True, vmem_limit_bytes=48 << 20),
    )(*[pltpu.with_memory_space_constraint(v, pltpu.HBM) for v in (inverse_blocks, coupling_blocks, deform_potential, shifts, emission_weight, absorption_weight, range_rows)])
    return pl.pallas_call(
        place,
        out_shape=(
            jax.ShapeDtypeStruct(landed.shape, BF16),
            jax.ShapeDtypeStruct((1,), F32),
        ),
        in_specs=[pl.BlockSpec(memory_space=pl.ANY)] * 2,
        out_specs=(hbm, hbm),
        scratch_shapes=[dma((NB + 1,))],
        compiler_params=pltpu.CompilerParams(vmem_limit_bytes=8 << 20),
    )(landed, total[0, :1])


def solution(mesh):
    in_specs = (
        P(None, "energy", "mom", None, None),
        P(None, "mom", None, None),
        P(),
        P(),
        P(),
        P(),
        P(),
    )
    out_specs = (P(None, "energy", "mom", None, None), P(("energy", "mom")))
    return jax.shard_map(body, mesh=mesh, in_specs=in_specs, out_specs=out_specs, check_vma=False)
```
